128 devices in a mesh: prow: 8 (over z, core), pcol: 16 (over y, x).
Axes of the slice: x: 4, y: 4, z: 4, core: 2. Of those that a mesh axis runs over, the one named last changes fastest.
Arguments:
- window_rhs: float32 [64, 8192], P(None, 'prow'), may hold values from -6 to 6
- past_solution: float32 [64, 32768], P(None, 'pcol'), may hold values from -6 to 6
- past_panel: float32 [8192, 32768], P('prow', 'pcol'), may hold values from -0.03125 to 0.03125
- window_panel: float32 [8, 1024, 16, 1024], P('prow', None, 'pcol'), may hold values from -0.09375 to 0.09375
- diag_inverse: float32 [8, 1024, 1024], P('prow'), may hold values from -1 to 1.5, as said below
- tile_list: int32 [128, 2], P(('prow', 'pcol')), may hold values from 0 to 63
- neighbor_list: int32 [128, 2, 8], P(('prow', 'pcol')), may hold values from 0 to 63
- force_constants: float32 [128, 2, 8, 128, 128], P(('prow', 'pcol')), may hold values from -0.1875 to 0.1875
Outputs:
- solution: float32 [64, 8192], P(None, 'prow')
- residual_forces: float32 [128, 2, 64, 128], P(('prow', 'pcol'))
The draws below stay inside these ranges and needn't reach their ends.
Inputs may be any that keep to these rules, and one draw needn't show every extreme that they name: `diag_inverse`: each block is lower triangular, with diagonal entries from 0.6 to 1.4.
All inputs are finite; a program needn't handle non-finite values.
Results may differ from the reference program's by a relative error of at most 0.00011.
Values sent between devices are 32-bit elements; how exact they have to be, the bound alone decides.
No kernel may reach another device: no remote copies, remote signals or barrier semaphores. Data moves between devices by JAX's collectives and lax.ppermute only.
A program may use at most 128 MiB of HBM per device.

```python
import jax
import jax.numpy as jnp
from jax import lax

NB = 1024
NRHS = 64
TILE = 128
NNB = 8
TPD = 2
WB = 8
COLS = 16
PAST = 32
TILES = 64
DEVICES = 128


def draw_diag_inverse(key, part):
    first, second = jax.random.split(key)
    lower = jax.random.normal(first, (WB, NB, NB), jnp.float32) * (0.6 / NB ** 0.5)
    lower = jnp.clip(lower, -0.9, 0.9)
    rows = jnp.arange(NB)[:, None]
    cols = jnp.arange(NB)[None, :]
    below = (rows > cols).astype(jnp.float32)
    same = (rows == cols).astype(jnp.float32)
    diagonal = jax.random.uniform(second, (WB, NB), jnp.float32, 0.6, 1.4)
    return lower * below[None] + diagonal[:, :, None] * same[None]


def touch_ends(array, key, smallest, high):
    dims = array.shape
    spot = [jax.random.randint(jax.random.fold_in(key, axis), (), 0, dims[axis]) for axis in range(len(dims))]
    array = array.at[tuple(spot)].set(smallest)
    longest = dims.index(max(dims))
    spot[longest] = (spot[longest] + 1) % dims[longest]
    return array.at[tuple(spot)].set(high)


def level_of(rng, extent, pieces, smallest, largest):
    level, own = 1.0, jax.random.fold_in(rng, 6)
    for axis_at, shards_of in pieces:
        heights = jnp.exp(jax.random.uniform(jax.random.fold_in(own, axis_at), (shards_of,), jnp.float32, smallest / len(pieces), largest / len(pieces)))
        level = level * jnp.repeat(heights, extent[axis_at] // shards_of).reshape([-1 if axis == axis_at else 1 for axis in range(len(extent))])
    return level


def scatter_about(own_key, dims, width, most, shards=(), kind=jnp.bfloat16):
    drawn = width * jax.random.normal(own_key, dims, jnp.float32)
    if shards:
        drawn = drawn * level_of(own_key, dims, shards, -0.22, 0.18)
    return jnp.clip(drawn, -most, most).astype(kind)


def setup_inputs(seed: int = 0) -> dict:
    seeds = jax.random.split(jax.random.key(seed), 9)
    return {
        "window_rhs": scatter_about(seeds[0], (NRHS, WB * NB), 1.0, 6.0, ((1, 8),), jnp.float32),
        "past_solution": scatter_about(seeds[1], (NRHS, PAST * NB), 1.0, 6.0, ((1, 16),), jnp.float32),
        "past_panel": scatter_about(seeds[2], (WB * NB, PAST * NB), (PAST * NB) ** -0.5, 0.03125, ((0, 8), (1, 16)), jnp.float32),
        "window_panel": scatter_about(seeds[3], (WB, NB, COLS, NB), (4 * NB) ** -0.5, 0.09375, ((0, 8), (2, 16)), jnp.float32),
        "diag_inverse": draw_diag_inverse(jax.random.fold_in(seeds[8], 71), 0),
        "tile_list": touch_ends(jax.random.randint(seeds[5], (DEVICES, TPD), 0, TILES), jax.random.fold_in(seeds[5], 1), 0, TILES - 1).astype(jnp.int32),
        "neighbor_list": touch_ends(jax.random.randint(seeds[6], (DEVICES, TPD, NNB), 0, TILES), jax.random.fold_in(seeds[6], 1), 0, TILES - 1).astype(jnp.int32),
        "force_constants": scatter_about(seeds[7], (DEVICES, TPD, NNB, TILE, TILE), (NNB * TILE) ** -0.5, 0.1875, ((0, 128),), jnp.float32),
    }


def reference(window_rhs, past_solution, past_panel, window_panel, diag_inverse, tile_list, neighbor_list, force_constants):
    highest = lax.Precision.HIGHEST
    past_terms = jnp.dot(past_solution, past_panel.T, precision=highest, preferred_element_type=jnp.float32)
    solved = []
    for k in range(WB):
        total = past_terms[:, k * NB:(k + 1) * NB]
        for j in range(k):
            total = total + jnp.dot(solved[j], window_panel[k, :, j, :].T, precision=highest, preferred_element_type=jnp.float32)
        diff = window_rhs[:, k * NB:(k + 1) * NB] - total
        solved.append(jnp.dot(diff, diag_inverse[k].T, precision=highest, preferred_element_type=jnp.float32))
    solution = jnp.concatenate(solved, axis=1)
    tiles = solution.reshape(NRHS, TILES, TILE)
    rhs_tiles = window_rhs.reshape(NRHS, TILES, TILE)
    near = tiles[:, neighbor_list]
    term = jnp.einsum("rdtnb,dtnab->dtra", near, force_constants, precision=highest)
    own = jnp.transpose(rhs_tiles[:, tile_list], (1, 2, 0, 3))
    return solution, own - term
```

```python
import jax
import jax.numpy as jnp
from jax import lax
from jax.experimental import pallas as pl
from jax.experimental.pallas import tpu as pltpu
from jax.sharding import Mesh
from jax.sharding import PartitionSpec as P

PROW = ("prow_0", "prow_1")
PCOL = ("pcol_0", "pcol_1")
EVERY = ("prow_0", "prow_1", "pcol_0", "pcol_1")
ROWS = 8
COLS = 16
HIGH = lax.Precision.HIGH


def product(left, right, left_dim, right_dim):
    return lax.dot_general(
        left,
        right,
        (((left_dim,), (right_dim,)), ((), ())),
        precision=HIGH,
        preferred_element_type=jnp.float32,
    )


def exchange(pieces, axes):
    return lax.all_to_all(pieces, axes, 0, 0, tiled=True)


def to_everyone(x, axes, count):
    return exchange(jnp.broadcast_to(x[None], (count, *x.shape)), axes)


def place(row, col):
    return row * COLS + col


def send(x, pairs):
    return lax.ppermute(x, EVERY, pairs)


def split_bf16(x):
    high = x.astype(jnp.bfloat16)
    low = (x - high.astype(jnp.float32)).astype(jnp.bfloat16)
    return high, low


def three_pass(left, right):
    dims = (((1,), (1,)), ((), ()))
    left_high, left_low = split_bf16(left)
    right_high, right_low = split_bf16(right)

    def one(a, b):
        return lax.dot_general(a, b, dims, preferred_element_type=jnp.float32)

    return one(left_high, right_high) + (one(left_high, right_low) + one(left_low, right_high))


def finish_kernel(tiles_ref, near_ref, row_ref, pieces_ref, rhs_ref, force_ref, solution_ref, residual_ref):
    row = row_ref[0]
    for group in range(8):
        for half in range(2):
            solution_ref[pl.ds(group * 8, 8), pl.ds(half * 512, 512)] = pieces_ref[row * COLS + group * 2 + half]
    for t in range(2):
        own = tiles_ref[t]
        total = rhs_ref[own // 8, :, pl.ds(pl.multiple_of((own % 8) * 128, 128), 128)]
        for n in range(8):
            tile = near_ref[t, n]
            block = tile // 8
            half = (tile % 8) // 4
            offset = pl.multiple_of((tile % 4) * 128, 128)
            near = jnp.concatenate(
                [pieces_ref[block * COLS + group * 2 + half, :, pl.ds(offset, 128)] for group in range(8)], axis=0
            )
            total = total - three_pass(near, force_ref[t, n])
        residual_ref[t] = total


def finish(tile_list, neighbor_list, row, pieces, rhs, force):
    vmem = pl.BlockSpec(memory_space=pltpu.VMEM)
    smem = pl.BlockSpec(memory_space=pltpu.SMEM)
    return pl.pallas_call(
        finish_kernel,
        out_shape=(
            jax.ShapeDtypeStruct((64, 1024), jnp.float32),
            jax.ShapeDtypeStruct((2, 64, 128), jnp.float32),
        ),
        in_specs=[smem, smem, smem, vmem, vmem, vmem],
        out_specs=(vmem, vmem),
        compiler_params=pltpu.CompilerParams(vmem_limit_bytes=32 * 1024 * 1024),
    )(tile_list, neighbor_list, row, pieces, rhs, force)


def per_device(
    window_rhs,
    past_solution,
    past_panel,
    window_panel,
    diag_inverse,
    tile_list,
    neighbor_list,
    force_constants,
):
    row = lax.axis_index(PROW)
    col = lax.axis_index(PCOL)
    block = window_panel[0, :, 0, :]
    inverse = diag_inverse[0]
    full_rhs = to_everyone(window_rhs, PROW, ROWS)

    past = product(past_solution, past_panel, 1, 1)
    past_rows = exchange(past.reshape(COLS, 4, 1024), PCOL).sum(axis=0)
    rhs_rows = lax.dynamic_slice_in_dim(window_rhs, col * 4, 4, 0)
    start_rows = product(rhs_rows - past_rows, inverse, 1, 1)
    start = to_everyone(start_rows, PCOL, COLS).reshape(64, 1024)

    weight = product(block, inverse, 0, 1)

    carried = start
    arrived = send(start, [(place(0, k - 1), place(k, 0)) for k in range(1, ROWS)])
    current = lax.cond(
        (col == 0) & (row > 0),
        lambda: carried - product(arrived, weight, 1, 0),
        lambda: carried,
    )
    for step in range(1, ROWS - 1):
        source = place(step, step - 1)
        parts = [send(current, [(source, place(k, step))]) for k in range(step + 1, ROWS)]
        partial = send(current, [(place(k, step - 1), place(k, step)) for k in range(step + 1, ROWS)])

        def fire(parts=parts, partial=partial):
            known = parts[0]
            for other in parts[1:]:
                known = known + other
            return partial - product(known, weight, 1, 0)

        current = lax.cond((col == step) & (row > step), fire, lambda current=current: current)

    pieces = current.reshape(8, 8, 2, 512).transpose(0, 2, 1, 3).reshape(COLS, 8, 512)
    spread = exchange(pieces, PCOL)
    own_piece = lax.dynamic_index_in_dim(spread, jnp.maximum(row - 1, 0), 0, keepdims=False)
    everything = to_everyone(own_piece, EVERY, ROWS * COLS)
    solution, residual = finish(
        tile_list[0], neighbor_list[0], row.reshape(1), everything, full_rhs, force_constants[0]
    )
    return (solution, residual[None])


def solution(mesh):
    torus = Mesh(mesh.devices.reshape(4, 2, 4, 4), EVERY)
    placed = (
        P(None, PROW),
        P(None, PCOL),
        P(PROW, PCOL),
        P(PROW, None, PCOL, None),
        P(PROW, None, None),
        P(EVERY, None),
        P(EVERY, None, None),
        P(EVERY, None, None, None, None),
    )
    return jax.shard_map(
        per_device,
        mesh=torus,
        in_specs=placed,
        out_specs=(P(None, PROW), P(EVERY, None, None, None)),
        check_vma=False,
    )
```

```python
import jax
import jax.numpy as jnp
from jax import lax
from jax.experimental import pallas as pl
from jax.experimental.pallas import tpu as pltpu
from jax.sharding import Mesh
from jax.sharding import PartitionSpec as P

PROW = ("prow_0", "prow_1")
PCOL = ("pcol_0", "pcol_1")
EVERY = ("prow_0", "prow_1", "pcol_0", "pcol_1")
ROWS = 8
COLS = 16
HIGH = lax.Precision.HIGH


def product(left, right, left_dim, right_dim):
    return lax.dot_general(
        left,
        right,
        (((left_dim,), (right_dim,)), ((), ())),
        precision=HIGH,
        preferred_element_type=jnp.float32,
    )


def exchange(pieces, axes):
    return lax.all_to_all(pieces, axes, 0, 0, tiled=True)


def to_everyone(x, axes, count):
    return exchange(jnp.broadcast_to(x[None], (count, *x.shape)), axes)


def place(row, col):
    return row * COLS + col


def send(x, pairs):
    return lax.ppermute(x, EVERY, pairs)


def split_bf16(x):
    high = x.astype(jnp.bfloat16)
    low = (x - high.astype(jnp.float32)).astype(jnp.bfloat16)
    return high, low


def three_pass(left, right_high, right_low):
    dims = (((1,), (1,)), ((), ()))
    left_high, left_low = split_bf16(left)
    rows = left.shape[0]
    both = lax.dot_general(
        jnp.concatenate([left_high, left_low], axis=0), right_high, dims, preferred_element_type=jnp.float32
    )
    return (both[:rows] + both[rows:]) + lax.dot_general(
        left_high, right_low, dims, preferred_element_type=jnp.float32
    )


VMEM = pl.BlockSpec(memory_space=pltpu.VMEM)
SMEM = pl.BlockSpec(memory_space=pltpu.SMEM)


def room(mib):
    return pltpu.CompilerParams(vmem_limit_bytes=mib * 1024 * 1024)


def form_kernel(inverse_ref, block_ref, inverse_high_ref, inverse_low_ref, high_ref, low_ref):
    @pl.when(pl.program_id(0) == 0)
    def _():
        inverse_high_ref[...], inverse_low_ref[...] = split_bf16(inverse_ref[...])

    count = block_ref.shape[0] // inverse_ref.shape[0]
    first = pl.program_id(0) * 2
    strips = [block_ref[pl.ds(first + i, inverse_ref.shape[0], stride=count), :] for i in range(2)]
    block_high, block_low = split_bf16(jnp.concatenate(strips, axis=1))

    def one(a, b):
        return jnp.dot(a, b, preferred_element_type=jnp.float32)

    total = one(inverse_high_ref[...], block_high)
    total = total + one(inverse_high_ref[...], block_low)
    total = total + one(inverse_low_ref[...], block_high)
    high_ref[...], low_ref[...] = split_bf16(total)


def form(inverse, block):
    order = inverse.shape[0]
    width = 256
    half = jax.ShapeDtypeStruct((order, order), jnp.bfloat16)
    whole = pl.BlockSpec((order, order), lambda i: (0, 0))
    strip = pl.BlockSpec((order, width), lambda i: (0, i))
    return pl.pallas_call(
        form_kernel,
        grid=(order // width,),
        in_specs=[whole, pl.BlockSpec(block.shape, lambda i: (0, 0))],
        out_specs=(whole, whole, strip, strip),
        out_shape=(half, half, half, half),
        compiler_params=room(24),
    )(inverse, block)


def start_kernel(rhs_ref, past_ref, high_ref, low_ref, out_ref):
    diff = rhs_ref[...] - past_ref[...]
    out_ref[...] = three_pass(diff, high_ref[...], low_ref[...])


def start_product(rhs, past, high, low):
    return pl.pallas_call(
        start_kernel,
        in_specs=[VMEM] * 4,
        out_specs=VMEM,
        out_shape=jax.ShapeDtypeStruct(rhs.shape, jnp.float32),
        compiler_params=room(4),
    )(rhs, past, high, low)


def fire(bases, knowns, high, low):
    count = len(bases)

    def kernel(*refs):
        total = refs[0][...]
        for ref in refs[1:count]:
            total = total + ref[...]
        known = refs[count][...]
        for ref in refs[count + 1 : -3]:
            known = known + ref[...]
        refs[-1][...] = total - three_pass(known, refs[-3][...], refs[-2][...])

    return pl.pallas_call(
        kernel,
        in_specs=[VMEM] * (count + len(knowns) + 2),
        out_specs=VMEM,
        out_shape=jax.ShapeDtypeStruct(knowns[0].shape, jnp.float32),
        compiler_params=room(8),
    )(*bases, *knowns, high, low)


def finish_kernel(tiles_ref, near_ref, row_ref, pieces_ref, *refs):
    rhs_refs, (force_ref, solution_ref, residual_ref) = refs[:-3], refs[-3:]
    row = row_ref[0]
    for group in range(8):
        for half in range(2):
            solution_ref[pl.ds(group * 8, 8), pl.ds(half * 512, 512)] = pieces_ref[row * COLS + group * 2 + half]
    for t in range(2):
        own = tiles_ref[t]
        own_row = own // 8
        behind = (row // 2 - own_row // 2 + 4) % 4
        core = (row + own_row) % 2
        for distance in range(4):

            @pl.when(behind == distance)
            def _():
                offset = pl.multiple_of((own % 8) * 128, 128)
                residual_ref[t] = rhs_refs[distance][core, :, pl.ds(offset, 128)]

        total = residual_ref[t]
        for n in range(8):
            tile = near_ref[t, n]
            block = tile // 8
            half = (tile % 8) // 4
            offset = pl.multiple_of((tile % 4) * 128, 128)
            near = jnp.concatenate(
                [pieces_ref[block * COLS + group * 2 + half, :, pl.ds(offset, 128)] for group in range(8)], axis=0
            )
            total = total - three_pass(near, *split_bf16(force_ref[t, n]))
        residual_ref[t] = total


def finish(tile_list, neighbor_list, row, pieces, rhs, force):
    return pl.pallas_call(
        finish_kernel,
        out_shape=(
            jax.ShapeDtypeStruct((64, 1024), jnp.float32),
            jax.ShapeDtypeStruct((2, 64, 128), jnp.float32),
        ),
        in_specs=[SMEM, SMEM, SMEM] + [VMEM] * (2 + len(rhs)),
        out_specs=(VMEM, VMEM),
        compiler_params=room(8),
    )(tile_list, neighbor_list, row, pieces, *rhs, force)


def per_device(
    window_rhs,
    past_solution,
    past_panel,
    window_panel,
    diag_inverse,
    tile_list,
    neighbor_list,
    force_constants,
):
    row = lax.axis_index(PROW)
    col = lax.axis_index(PCOL)
    block = window_panel.reshape(-1, 128)
    inverse = diag_inverse[0]

    other_rhs = lax.ppermute(window_rhs, "prow_1", [(0, 1), (1, 0)])
    pair = jnp.stack([window_rhs, other_rhs])
    full_rhs = [pair] + [lax.ppermute(pair, "prow_0", [(i, (i + d) % 4) for i in range(4)]) for d in (1, 2, 3)]

    past = product(past_solution, past_panel, 1, 1)
    past_rows = exchange(past.reshape(COLS, 4, 1024), PCOL).sum(axis=0)
    inverse_high, inverse_low, high, low = form(inverse, block)
    rhs_rows = lax.dynamic_slice_in_dim(window_rhs, col * 4, 4, 0)
    start_rows = start_product(rhs_rows, past_rows, inverse_high, inverse_low)
    start = to_everyone(start_rows, PCOL, COLS).reshape(64, 1024)
    start, *full_rhs = lax.optimization_barrier((start, *full_rhs))

    total = jnp.where(row == col + 1, start, jnp.zeros_like(start))
    arrived = send(start, [(place(0, k - 1), place(k, 0)) for k in range(1, ROWS)])
    current = lax.cond(
        (col == 0) & (row > 0),
        lambda: fire([total], [arrived], high, low),
        lambda: start,
    )
    for step in range(1, ROWS - 1):
        source = place(step, step - 1)
        beside = place(step ^ 1, step - 1)
        knowns = [send(current, [(source, place(step + 1, step))])]
        if step + 2 < ROWS:
            relayed = send(current, [(source, beside)])
            knowns += [send(relayed, [(beside, place(k, step))]) for k in range(step + 2, ROWS)]
        extra = send(current, [(place(k, step - 1), place(k, k - 1)) for k in range(step + 1, ROWS)])
        current = lax.cond(
            (col == step) & (row > step),
            lambda: fire([total, extra], knowns, high, low),
            lambda: current,
        )
        total = total + extra

    pieces = current.reshape(8, 8, 2, 512).transpose(0, 2, 1, 3).reshape(COLS, 8, 512)
    spread = exchange(pieces, PCOL)
    own_piece = lax.dynamic_index_in_dim(spread, jnp.maximum(row - 1, 0), 0, keepdims=False)
    everything = to_everyone(own_piece, EVERY, ROWS * COLS)
    solution, residual = finish(
        tile_list[0], neighbor_list[0], row.reshape(1), everything, full_rhs, force_constants[0]
    )
    return (solution, residual[None])


def solution(mesh):
    torus = Mesh(mesh.devices.reshape(4, 2, 4, 4), EVERY)
    placed = (
        P(None, PROW),
        P(None, PCOL),
        P(PROW, PCOL),
        P(PROW, None, PCOL, None),
        P(PROW, None, None),
        P(EVERY, None),
        P(EVERY, None, None),
        P(EVERY, None, None, None, None),
    )
    return jax.shard_map(
        per_device,
        mesh=torus,
        in_specs=placed,
        out_specs=(P(None, PROW), P(EVERY, None, None, None)),
        check_vma=False,
    )
```

```python
import jax
import jax.numpy as jnp
from jax import lax
from jax.experimental import pallas as pl
from jax.experimental.pallas import tpu as pltpu
from jax.sharding import Mesh
from jax.sharding import PartitionSpec as P

PROW = ("prow_0", "prow_1")
PCOL = ("pcol_0", "pcol_1")
EVERY = ("prow_0", "prow_1", "pcol_0", "pcol_1")
ROWS = 8
COLS = 16
HIGH = lax.Precision.HIGH


def product(left, right, left_dim, right_dim):
    return lax.dot_general(
        left,
        right,
        (((left_dim,), (right_dim,)), ((), ())),
        precision=HIGH,
        preferred_element_type=jnp.float32,
    )


def exchange(pieces, axes):
    return lax.all_to_all(pieces, axes, 0, 0, tiled=True)


def to_everyone(x, axes, count):
    return exchange(jnp.broadcast_to(x[None], (count, *x.shape)), axes)


def place(row, col):
    return row * COLS + col


def send(x, pairs):
    return lax.ppermute(x, EVERY, pairs)


def split_bf16(x):
    high = x.astype(jnp.bfloat16)
    low = (x - high.astype(jnp.float32)).astype(jnp.bfloat16)
    return high, low


ACROSS = (((1,), (1,)), ((), ()))


def high_passes(left, right_high):
    left_high, left_low = split_bf16(left)
    rows = left.shape[0]
    both = lax.dot_general(
        jnp.concatenate([left_high, left_low], axis=0), right_high, ACROSS, preferred_element_type=jnp.float32
    )
    return both[:rows] + both[rows:]


def low_pass(left, right_low):
    return lax.dot_general(left.astype(jnp.bfloat16), right_low, ACROSS, preferred_element_type=jnp.float32)


def three_pass(left, right_high, right_low):
    return high_passes(left, right_high) + low_pass(left, right_low)


VMEM = pl.BlockSpec(memory_space=pltpu.VMEM)
SMEM = pl.BlockSpec(memory_space=pltpu.SMEM)


def room(mib):
    return pltpu.CompilerParams(vmem_limit_bytes=mib * 1024 * 1024)


def in_hbm(x):
    return pltpu.with_memory_space_constraint(x, pltpu.HBM)


def in_vmem(x):
    return pltpu.with_memory_space_constraint(x, pltpu.VMEM)


PARTS = 4


def form_kernel(
    inverse_hbm,
    block_hbm,
    high_ref,
    low_ref,
    inverse_buffer,
    block_buffer,
    block_high_ref,
    block_low_ref,
    inverse_sems,
    block_sems,
):
    order = inverse_buffer.shape[0]
    part = order // PARTS
    lines = block_buffer.shape[0] // PARTS
    count = lines // part

    def block_copy(i):
        span = pl.ds(i * lines, lines)
        return pltpu.make_async_copy(block_hbm.at[span], block_buffer.at[span], block_sems.at[i])

    def inverse_copy(i):
        span = pl.ds(i * part, part)
        return pltpu.make_async_copy(inverse_hbm.at[span], inverse_buffer.at[span], inverse_sems.at[i])

    for i in range(PARTS):
        block_copy(i).start()
    for i in range(PARTS):
        inverse_copy(i).start()
    for i in range(PARTS):
        block_copy(i).wait()
        span = pl.ds(i * part, part)
        for j in range(count):
            lanes = pl.ds(j * 128, 128)
            strip = block_buffer[pl.ds(i * lines + j, part, stride=count), :]
            block_high_ref[span, lanes], block_low_ref[span, lanes] = split_bf16(strip)

    def one(a, b):
        return jnp.dot(a, b, preferred_element_type=jnp.float32)

    for i in range(PARTS):
        inverse_copy(i).wait()
        span = pl.ds(i * part, part)
        inverse_high, inverse_low = split_bf16(inverse_buffer[span, :])
        total = one(inverse_high, block_high_ref[...])
        total = total + one(inverse_high, block_low_ref[...])
        total = total + one(inverse_low, block_high_ref[...])
        high_ref[span, :], low_ref[span, :] = split_bf16(total)


def form(inverse, block):
    order = inverse.shape[0]
    half = jax.ShapeDtypeStruct((order, order), jnp.bfloat16)
    hbm = pl.BlockSpec(memory_space=pltpu.HBM)
    return pl.pallas_call(
        form_kernel,
        in_specs=[hbm, hbm],
        out_specs=(VMEM,) * 2,
        out_shape=(half,) * 2,
        scratch_shapes=[
            pltpu.VMEM(inverse.shape, jnp.float32),
            pltpu.VMEM(block.shape, jnp.float32),
            pltpu.VMEM((order, order), jnp.bfloat16),
            pltpu.VMEM((order, order), jnp.bfloat16),
            pltpu.SemaphoreType.DMA((PARTS,)),
            pltpu.SemaphoreType.DMA((PARTS,)),
        ],
        compiler_params=room(24),
    )(in_hbm(inverse), in_hbm(block))


def start_kernel(rhs_ref, past_ref, inverse_hbm, out_ref, buffer, sems):
    part = buffer.shape[0] // PARTS

    def copy(i):
        span = pl.ds(i * part, part)
        return pltpu.make_async_copy(inverse_hbm.at[span], buffer.at[span], sems.at[i])

    for i in range(PARTS):
        copy(i).start()
    diff = rhs_ref[...] - past_ref[...]
    for i in range(PARTS):
        copy(i).wait()
        span = pl.ds(i * part, part)
        out_ref[:, span] = three_pass(diff, *split_bf16(buffer[span, :]))


def start_product(rhs, past, inverse):
    return pl.pallas_call(
        start_kernel,
        in_specs=[VMEM, VMEM, pl.BlockSpec(memory_space=pltpu.HBM)],
        out_specs=VMEM,
        out_shape=jax.ShapeDtypeStruct(rhs.shape, jnp.float32),
        scratch_shapes=[pltpu.VMEM(inverse.shape, jnp.float32), pltpu.SemaphoreType.DMA((PARTS,))],
        compiler_params=room(12),
    )(rhs, past, in_hbm(inverse))


def fire(bases, knowns, high, low):
    count = len(bases)

    def kernel(*refs):
        base_refs, known_refs = refs[:count], refs[count:-5]
        high_ref, low_hbm, out_ref, low_buffer, sem = refs[-5:]
        copy = pltpu.make_async_copy(low_hbm, low_buffer, sem)
        copy.start()
        total = base_refs[0][...]
        for ref in base_refs[1:]:
            total = total + ref[...]
        known = known_refs[0][...]
        for ref in known_refs[1:]:
            known = known + ref[...]
        total = total - high_passes(known, high_ref[...])
        copy.wait()
        out_ref[...] = total - low_pass(known, low_buffer[...])

    return pl.pallas_call(
        kernel,
        in_specs=[VMEM] * (count + len(knowns) + 1) + [pl.BlockSpec(memory_space=pltpu.HBM)],
        out_specs=VMEM,
        out_shape=jax.ShapeDtypeStruct(knowns[0].shape, jnp.float32),
        scratch_shapes=[pltpu.VMEM(low.shape, low.dtype), pltpu.SemaphoreType.DMA],
        compiler_params=room(10),
    )(*bases, *knowns, high, in_hbm(low))


def finish_kernel(tiles_ref, near_ref, row_ref, pieces_ref, *refs):
    rhs_refs, (force_ref, solution_ref, residual_ref) = refs[:-3], refs[-3:]
    row = row_ref[0]
    for group in range(8):
        for half in range(2):
            solution_ref[pl.ds(group * 8, 8), pl.ds(half * 512, 512)] = pieces_ref[row * COLS + group * 2 + half]
    for t in range(2):
        own = tiles_ref[t]
        own_row = own // 8
        behind = (row // 2 - own_row // 2 + 4) % 4
        core = (row + own_row) % 2
        for distance in range(4):

            @pl.when(behind == distance)
            def _():
                offset = pl.multiple_of((own % 8) * 128, 128)
                residual_ref[t] = rhs_refs[distance][core, :, pl.ds(offset, 128)]

        total = residual_ref[t]
        for n in range(8):
            tile = near_ref[t, n]
            block = tile // 8
            half = (tile % 8) // 4
            offset = pl.multiple_of((tile % 4) * 128, 128)
            near = jnp.concatenate(
                [pieces_ref[block * COLS + group * 2 + half, :, pl.ds(offset, 128)] for group in range(8)], axis=0
            )
            total = total - three_pass(near, *split_bf16(force_ref[t, n]))
        residual_ref[t] = total


def finish(tile_list, neighbor_list, row, pieces, rhs, force):
    return pl.pallas_call(
        finish_kernel,
        out_shape=(
            jax.ShapeDtypeStruct((64, 1024), jnp.float32),
            jax.ShapeDtypeStruct((2, 64, 128), jnp.float32),
        ),
        in_specs=[SMEM, SMEM, SMEM] + [VMEM] * (2 + len(rhs)),
        out_specs=(VMEM, VMEM),
        compiler_params=room(8),
    )(tile_list, neighbor_list, row, pieces, *rhs, force)


def per_device(
    window_rhs,
    past_solution,
    past_panel,
    window_panel,
    diag_inverse,
    tile_list,
    neighbor_list,
    force_constants,
):
    row = lax.axis_index(PROW)
    col = lax.axis_index(PCOL)
    block = window_panel.reshape(-1, 128)
    inverse = diag_inverse[0]

    other_rhs = lax.ppermute(window_rhs, "prow_1", [(0, 1), (1, 0)])
    pair = jnp.stack([window_rhs, other_rhs])

    def around(x, distance):
        return lax.ppermute(x, "prow_0", [(i, (i + distance) % 4) for i in range(4)])

    next_rhs = around(pair, 1)
    past = product(past_solution, past_panel, 1, 1)
    past, pair, next_rhs = lax.optimization_barrier((past, pair, next_rhs))
    last_rhs = around(pair, 3)
    past_rows = exchange(past.reshape(COLS, 4, 1024), PCOL).sum(axis=0)
    high, low = form(inverse, block)
    high = in_vmem(high)
    past_rows, pair, last_rhs, high = lax.optimization_barrier((past_rows, pair, last_rhs, high))
    far_rhs = around(pair, 2)
    rhs_rows = lax.dynamic_slice_in_dim(window_rhs, col * 4, 4, 0)
    start_rows = start_product(rhs_rows, past_rows, inverse)
    start = to_everyone(start_rows, PCOL, COLS).reshape(64, 1024)
    start, far_rhs = lax.optimization_barrier((start, far_rhs))
    full_rhs = [pair, next_rhs, far_rhs, last_rhs]

    total = jnp.where(row == col + 1, start, jnp.zeros_like(start))
    arrived = send(start, [(place(0, k - 1), place(k, 0)) for k in range(1, ROWS)])
    current = lax.cond(
        (col == 0) & (row > 0),
        lambda: fire([total], [arrived], high, low),
        lambda: start,
    )
    for step in range(1, ROWS - 1):
        source = place(step, step - 1)
        beside = place(step ^ 1, step - 1)
        knowns = [send(current, [(source, place(step + 1, step))])]
        if step + 2 < ROWS:
            relayed = send(current, [(source, beside)])
            knowns += [send(relayed, [(beside, place(k, step))]) for k in range(step + 2, ROWS)]
        extra = send(current, [(place(k, step - 1), place(k, k - 1)) for k in range(step + 1, ROWS)])
        current = lax.cond(
            (col == step) & (row > step),
            lambda: fire([total, extra], knowns, high, low),
            lambda: current,
        )
        total = total + extra

    pieces = current.reshape(8, 8, 2, 512).transpose(0, 2, 1, 3).reshape(COLS, 8, 512)
    spread = exchange(pieces, PCOL)
    own_piece = lax.dynamic_index_in_dim(spread, jnp.maximum(row - 1, 0), 0, keepdims=False)
    everything = to_everyone(own_piece, EVERY, ROWS * COLS)
    solution, residual = finish(
        tile_list[0], neighbor_list[0], row.reshape(1), everything, full_rhs, force_constants[0]
    )
    return (solution, residual[None])


def solution(mesh):
    torus = Mesh(mesh.devices.reshape(4, 2, 4, 4), EVERY)
    placed = (
        P(None, PROW),
        P(None, PCOL),
        P(PROW, PCOL),
        P(PROW, None, PCOL, None),
        P(PROW, None, None),
        P(EVERY, None),
        P(EVERY, None, None),
        P(EVERY, None, None, None, None),
    )
    return jax.shard_map(
        per_device,
        mesh=torus,
        in_specs=placed,
        out_specs=(P(None, PROW), P(EVERY, None, None, None)),
        check_vma=False,
    )
```

```python
import jax
import jax.numpy as jnp
from jax import lax
from jax.experimental import pallas as pl
from jax.experimental.pallas import tpu as pltpu
from jax.sharding import Mesh
from jax.sharding import PartitionSpec as P

PROW = ("prow_0", "prow_1")
PCOL = ("pcol_0", "pcol_1")
EVERY = ("prow_0", "prow_1", "pcol_0", "pcol_1")
ROWS = 8
COLS = 16
HIGH = lax.Precision.HIGH


def product(left, right, left_dim, right_dim):
    return lax.dot_general(
        left,
        right,
        (((left_dim,), (right_dim,)), ((), ())),
        precision=HIGH,
        preferred_element_type=jnp.float32,
    )


def exchange(pieces, axes):
    return lax.all_to_all(pieces, axes, 0, 0, tiled=True)


def to_everyone(x, axes, count):
    return exchange(jnp.broadcast_to(x[None], (count, *x.shape)), axes)


def place(row, col):
    return row * COLS + col


def send(x, pairs):
    return lax.ppermute(x, EVERY, pairs)


def split_bf16(x):
    high = x.astype(jnp.bfloat16)
    low = (x - high.astype(jnp.float32)).astype(jnp.bfloat16)
    return high, low


ACROSS = (((1,), (1,)), ((), ()))
ALONG = (((1,), (0,)), ((), ()))


def high_passes(left, right_high, dims):
    left_high, left_low = split_bf16(left)
    rows = left.shape[0]
    both = lax.dot_general(
        jnp.concatenate([left_high, left_low], axis=0), right_high, dims, preferred_element_type=jnp.float32
    )
    return both[:rows] + both[rows:]


def low_pass(left, right_low, dims):
    return lax.dot_general(left.astype(jnp.bfloat16), right_low, dims, preferred_element_type=jnp.float32)


def three_pass(left, right_high, right_low, dims=ACROSS):
    return high_passes(left, right_high, dims) + low_pass(left, right_low, dims)


VMEM = pl.BlockSpec(memory_space=pltpu.VMEM)
SMEM = pl.BlockSpec(memory_space=pltpu.SMEM)


def room(mib):
    return pltpu.CompilerParams(vmem_limit_bytes=mib * 1024 * 1024)


def in_hbm(x):
    return pltpu.with_memory_space_constraint(x, pltpu.HBM)


def in_vmem(x):
    return pltpu.with_memory_space_constraint(x, pltpu.VMEM)


PARTS = 4


def form_kernel(
    inverse_hbm,
    block_hbm,
    high_ref,
    low_ref,
    inverse_buffer,
    block_buffer,
    block_high_ref,
    block_low_ref,
    inverse_sems,
    block_sems,
):
    order = inverse_buffer.shape[0]
    part = order // PARTS
    lines = block_buffer.shape[0] // PARTS
    count = lines // part

    def block_copy(i):
        span = pl.ds(i * lines, lines)
        return pltpu.make_async_copy(block_hbm.at[span], block_buffer.at[span], block_sems.at[i])

    def inverse_copy(i):
        span = pl.ds(i * part, part)
        return pltpu.make_async_copy(inverse_hbm.at[span], inverse_buffer.at[span], inverse_sems.at[i])

    for i in range(PARTS):
        block_copy(i).start()
    for i in range(PARTS):
        inverse_copy(i).start()
    for i in range(PARTS):
        block_copy(i).wait()
        span = pl.ds(i * part, part)
        for j in range(count):
            lanes = pl.ds(j * 128, 128)
            strip = block_buffer[pl.ds(i * lines + j, part, stride=count), :]
            block_high_ref[span, lanes], block_low_ref[span, lanes] = split_bf16(strip)

    def one(a, b):
        return jnp.dot(a, b, preferred_element_type=jnp.float32)

    for i in range(PARTS):
        inverse_copy(i).wait()
        span = pl.ds(i * part, part)
        inverse_high, inverse_low = split_bf16(inverse_buffer[span, :])
        total = one(inverse_high, block_high_ref[...])
        total = total + one(inverse_high, block_low_ref[...])
        total = total + one(inverse_low, block_high_ref[...])
        high_ref[:, span], low_ref[:, span] = split_bf16(total.T)


def form(inverse, block):
    order = inverse.shape[0]
    half = jax.ShapeDtypeStruct((order, order), jnp.bfloat16)
    hbm = pl.BlockSpec(memory_space=pltpu.HBM)
    return pl.pallas_call(
        form_kernel,
        in_specs=[hbm, hbm],
        out_specs=(VMEM,) * 2,
        out_shape=(half,) * 2,
        scratch_shapes=[
            pltpu.VMEM(inverse.shape, jnp.float32),
            pltpu.VMEM(block.shape, jnp.float32),
            pltpu.VMEM((order, order), jnp.bfloat16),
            pltpu.VMEM((order, order), jnp.bfloat16),
            pltpu.SemaphoreType.DMA((PARTS,)),
            pltpu.SemaphoreType.DMA((PARTS,)),
        ],
        compiler_params=room(24),
    )(in_hbm(inverse), in_hbm(block))


def start_kernel(rhs_ref, past_ref, inverse_hbm, out_ref, buffer, sems):
    part = buffer.shape[0] // PARTS

    def copy(i):
        span = pl.ds(i * part, part)
        return pltpu.make_async_copy(inverse_hbm.at[span], buffer.at[span], sems.at[i])

    for i in range(PARTS):
        copy(i).start()
    diff = rhs_ref[...] - past_ref[...]
    for i in range(PARTS):
        copy(i).wait()
        span = pl.ds(i * part, part)
        out_ref[:, span] = three_pass(diff, *split_bf16(buffer[span, :]))


def start_product(rhs, past, inverse):
    return pl.pallas_call(
        start_kernel,
        in_specs=[VMEM, VMEM, pl.BlockSpec(memory_space=pltpu.HBM)],
        out_specs=VMEM,
        out_shape=jax.ShapeDtypeStruct(rhs.shape, jnp.float32),
        scratch_shapes=[pltpu.VMEM(inverse.shape, jnp.float32), pltpu.SemaphoreType.DMA((PARTS,))],
        compiler_params=room(12),
    )(rhs, past, in_hbm(inverse))


def fire(step, where, before, total, extra, knowns, high, low):
    def kernel(where_ref, before_ref, total_ref, *refs):
        row, col = where_ref[0], where_ref[1]
        turn = jnp.logical_and(col == step, row > step)
        known_refs = refs[: len(knowns)]
        extra_refs = refs[len(knowns) : -4]
        high_ref, low_ref, out_ref, sum_ref = refs[-4:]
        if extra_refs:
            sum_ref[...] = total_ref[...] + extra_refs[0][...]
        else:
            sum_ref[...] = jnp.where(row == col + 1, total_ref[...], 0.0)

        @pl.when(jnp.logical_not(turn))
        def _():
            out_ref[...] = before_ref[...]

        @pl.when(turn)
        def _():
            known = known_refs[0][...]
            for ref in known_refs[1:]:
                known = known + ref[...]
            out_ref[...] = sum_ref[...] - three_pass(known, high_ref[...], low_ref[...], ALONG)

    extras = [] if extra is None else [extra]
    like = jax.ShapeDtypeStruct(before.shape, jnp.float32)
    return pl.pallas_call(
        kernel,
        in_specs=[SMEM] + [VMEM] * (len(knowns) + len(extras) + 4),
        out_specs=(VMEM, VMEM),
        out_shape=(like, like),
        compiler_params=room(3),
    )(where, before, total, *knowns, *extras, high, low)


def finish_kernel(tiles_ref, near_ref, row_ref, pieces_ref, rhs_ref, force_ref, solution_ref, residual_ref):
    row = row_ref[0]
    for group in range(8):
        for half in range(2):
            solution_ref[pl.ds(group * 8, 8), pl.ds(half * 512, 512)] = pieces_ref[row * COLS + group * 2 + half]
    for t in range(2):
        own = tiles_ref[t]
        total = rhs_ref[own // 8, :, pl.ds(pl.multiple_of((own % 8) * 128, 128), 128)]
        for n in range(8):
            tile = near_ref[t, n]
            block = tile // 8
            half = (tile % 8) // 4
            offset = pl.multiple_of((tile % 4) * 128, 128)
            near = jnp.concatenate(
                [pieces_ref[block * COLS + group * 2 + half, :, pl.ds(offset, 128)] for group in range(8)], axis=0
            )
            total = total - three_pass(near, *split_bf16(force_ref[t, n]))
        residual_ref[t] = total


def finish(tile_list, neighbor_list, row, pieces, rhs, force):
    return pl.pallas_call(
        finish_kernel,
        out_shape=(
            jax.ShapeDtypeStruct((64, 1024), jnp.float32),
            jax.ShapeDtypeStruct((2, 64, 128), jnp.float32),
        ),
        in_specs=[SMEM, SMEM, SMEM] + [VMEM] * 3,
        out_specs=(VMEM, VMEM),
        compiler_params=room(8),
    )(tile_list, neighbor_list, row, pieces, rhs, force)


def per_device(
    window_rhs,
    past_solution,
    past_panel,
    window_panel,
    diag_inverse,
    tile_list,
    neighbor_list,
    force_constants,
):
    row = lax.axis_index(PROW)
    col = lax.axis_index(PCOL)
    block = window_panel.reshape(-1, 128)
    where = jnp.stack([row, col]).astype(jnp.int32)
    inverse = diag_inverse[0]

    full_rhs = lax.all_gather(window_rhs, PROW, axis=0, tiled=False)
    past = product(past_solution, past_panel, 1, 1)
    past_rows = exchange(past.reshape(COLS, 4, 1024), PCOL).sum(axis=0)
    high, low = (in_vmem(x) for x in form(inverse, block))
    past_rows, high = lax.optimization_barrier((past_rows, high))
    rhs_rows = lax.dynamic_slice_in_dim(window_rhs, col * 4, 4, 0)
    start_rows = start_product(rhs_rows, past_rows, inverse)
    start = to_everyone(start_rows, PCOL, COLS).reshape(64, 1024)

    arrived = send(start, [(place(0, k - 1), place(k, 0)) for k in range(1, ROWS)])
    current, total = fire(0, where, start, start, None, [arrived], high, low)
    for step in range(1, ROWS - 1):
        source = place(step, step - 1)
        beside = place(step ^ 1, step - 1)
        knowns = [send(current, [(source, place(step + 1, step))])]
        if step + 2 < ROWS:
            relayed = send(current, [(source, beside)])
            knowns += [send(relayed, [(beside, place(k, step))]) for k in range(step + 2, ROWS)]
        extra = send(current, [(place(k, step - 1), place(k, k - 1)) for k in range(step + 1, ROWS)])
        current, total = fire(step, where, current, total, extra, knowns, high, low)

    pieces = current.reshape(8, 8, 2, 512).transpose(0, 2, 1, 3).reshape(COLS, 8, 512)
    spread = exchange(pieces, PCOL)
    own_piece = lax.dynamic_index_in_dim(spread, jnp.maximum(row - 1, 0), 0, keepdims=False)
    everything = to_everyone(own_piece, EVERY, ROWS * COLS)
    solution, residual = finish(
        tile_list[0], neighbor_list[0], where, everything, full_rhs, force_constants[0]
    )
    return (solution, residual[None])


def solution(mesh):
    torus = Mesh(mesh.devices.reshape(4, 2, 4, 4), EVERY)
    placed = (
        P(None, PROW),
        P(None, PCOL),
        P(PROW, PCOL),
        P(PROW, None, PCOL, None),
        P(PROW, None, None),
        P(EVERY, None),
        P(EVERY, None, None),
        P(EVERY, None, None, None, None),
    )
    return jax.shard_map(
        per_device,
        mesh=torus,
        in_specs=placed,
        out_specs=(P(None, PROW), P(EVERY, None, None, None)),
        check_vma=False,
    )
```

```python
import jax
import jax.numpy as jnp
from jax import lax
from jax.experimental import pallas as pl
from jax.experimental.pallas import tpu as pltpu
from jax.sharding import Mesh
from jax.sharding import PartitionSpec as P

PROW = ("prow_0", "prow_1")
PCOL = ("pcol_0", "pcol_1")
EVERY = ("prow_0", "prow_1", "pcol_0", "pcol_1")
ROWS = 8
COLS = 16
HIGH = lax.Precision.HIGH


def product(left, right, left_dim, right_dim):
    return lax.dot_general(
        left,
        right,
        (((left_dim,), (right_dim,)), ((), ())),
        precision=HIGH,
        preferred_element_type=jnp.float32,
    )


def exchange(pieces, axes):
    return lax.all_to_all(pieces, axes, 0, 0, tiled=True)


def to_everyone(x, axes, count):
    return exchange(jnp.broadcast_to(x[None], (count, *x.shape)), axes)


def place(row, col):
    return row * COLS + col


def send(x, pairs):
    return lax.ppermute(x, EVERY, pairs)


def split_bf16(x):
    high = x.astype(jnp.bfloat16)
    low = (x - high.astype(jnp.float32)).astype(jnp.bfloat16)
    return high, low


ACROSS = (((1,), (1,)), ((), ()))
ALONG = (((1,), (0,)), ((), ()))


def high_passes(left, right_high, dims):
    left_high, left_low = split_bf16(left)
    rows = left.shape[0]
    both = lax.dot_general(
        jnp.concatenate([left_high, left_low], axis=0), right_high, dims, preferred_element_type=jnp.float32
    )
    return both[:rows] + both[rows:]


def low_pass(left, right_low, dims):
    return lax.dot_general(left.astype(jnp.bfloat16), right_low, dims, preferred_element_type=jnp.float32)


def three_pass(left, right_high, right_low, dims=ACROSS):
    return high_passes(left, right_high, dims) + low_pass(left, right_low, dims)


VMEM = pl.BlockSpec(memory_space=pltpu.VMEM)
SMEM = pl.BlockSpec(memory_space=pltpu.SMEM)


def room(mib):
    return pltpu.CompilerParams(vmem_limit_bytes=mib * 1024 * 1024)


def in_hbm(x):
    return pltpu.with_memory_space_constraint(x, pltpu.HBM)


def in_vmem(x):
    return pltpu.with_memory_space_constraint(x, pltpu.VMEM)


PARTS = 4


def form_kernel(
    inverse_hbm,
    block_hbm,
    high_ref,
    low_ref,
    inverse_buffer,
    block_buffer,
    block_high_ref,
    block_low_ref,
    inverse_sems,
    block_sems,
):
    order = inverse_buffer.shape[0]
    part = order // PARTS
    lines = block_buffer.shape[0] // PARTS
    count = lines // part

    def block_copy(i):
        span = pl.ds(i * lines, lines)
        return pltpu.make_async_copy(block_hbm.at[span], block_buffer.at[span], block_sems.at[i])

    def inverse_copy(i):
        span = pl.ds(i * part, part)
        return pltpu.make_async_copy(inverse_hbm.at[span], inverse_buffer.at[span], inverse_sems.at[i])

    for i in range(PARTS):
        block_copy(i).start()
    for i in range(PARTS):
        inverse_copy(i).start()
    for i in range(PARTS):
        block_copy(i).wait()
        span = pl.ds(i * part, part)
        for j in range(count):
            lanes = pl.ds(j * 128, 128)
            strip = block_buffer[pl.ds(i * lines + j, part, stride=count), :]
            block_high_ref[span, lanes], block_low_ref[span, lanes] = split_bf16(strip)

    def one(a, b):
        return jnp.dot(a, b, preferred_element_type=jnp.float32)

    for i in range(PARTS):
        inverse_copy(i).wait()
        span = pl.ds(i * part, part)
        inverse_high, inverse_low = split_bf16(inverse_buffer[span, :])
        total = one(inverse_high, block_high_ref[...])
        total = total + one(inverse_high, block_low_ref[...])
        total = total + one(inverse_low, block_high_ref[...])
        high_ref[:, span], low_ref[:, span] = split_bf16(total.T)


def form(inverse, block):
    order = inverse.shape[0]
    half = jax.ShapeDtypeStruct((order, order), jnp.bfloat16)
    hbm = pl.BlockSpec(memory_space=pltpu.HBM)
    return pl.pallas_call(
        form_kernel,
        in_specs=[hbm, hbm],
        out_specs=(VMEM,) * 2,
        out_shape=(half,) * 2,
        scratch_shapes=[
            pltpu.VMEM(inverse.shape, jnp.float32),
            pltpu.VMEM(block.shape, jnp.float32),
            pltpu.VMEM((order, order), jnp.bfloat16),
            pltpu.VMEM((order, order), jnp.bfloat16),
            pltpu.SemaphoreType.DMA((PARTS,)),
            pltpu.SemaphoreType.DMA((PARTS,)),
        ],
        compiler_params=room(24),
    )(in_hbm(inverse), in_hbm(block))


def start_kernel(rhs_ref, past_ref, inverse_hbm, out_ref, buffer, sems):
    part = buffer.shape[0] // PARTS

    def copy(i):
        span = pl.ds(i * part, part)
        return pltpu.make_async_copy(inverse_hbm.at[span], buffer.at[span], sems.at[i])

    for i in range(PARTS):
        copy(i).start()
    diff = rhs_ref[...] - past_ref[...]
    for i in range(PARTS):
        copy(i).wait()
        span = pl.ds(i * part, part)
        out_ref[:, span] = three_pass(diff, *split_bf16(buffer[span, :]))


def start_product(rhs, past, inverse):
    return pl.pallas_call(
        start_kernel,
        in_specs=[VMEM, VMEM, pl.BlockSpec(memory_space=pltpu.HBM)],
        out_specs=VMEM,
        out_shape=jax.ShapeDtypeStruct(rhs.shape, jnp.float32),
        scratch_shapes=[pltpu.VMEM(inverse.shape, jnp.float32), pltpu.SemaphoreType.DMA((PARTS,))],
        compiler_params=room(12),
    )(rhs, past, in_hbm(inverse))


def fire(step, where, before, total, extras, knowns, high, low):
    def kernel(where_ref, before_ref, total_ref, *refs):
        row, col = where_ref[0], where_ref[1]
        turn = jnp.logical_and(col == step, row > step)
        known_refs = refs[: len(knowns)]
        extra_refs = refs[len(knowns) : -4]
        high_ref, low_ref, out_ref, sum_ref = refs[-4:]
        if extra_refs:
            total = total_ref[...]
            for ref in extra_refs:
                total = total + ref[...]
            sum_ref[...] = total
        else:
            sum_ref[...] = jnp.where(row == col + 1, total_ref[...], 0.0)

        @pl.when(jnp.logical_not(turn))
        def _():
            out_ref[...] = before_ref[...]

        @pl.when(jnp.logical_and(turn, row == step + 1))
        def _():
            out_ref[...] = known_refs[0][...]

        @pl.when(jnp.logical_and(turn, row > step + 1))
        def _():
            known = known_refs[0][...]
            for ref in known_refs[1:]:
                known = known + ref[...]
            out_ref[...] = known

        @pl.when(turn)
        def _():
            out_ref[...] = sum_ref[...] - three_pass(out_ref[...], high_ref[...], low_ref[...], ALONG)

    like = jax.ShapeDtypeStruct(before.shape, jnp.float32)
    return pl.pallas_call(
        kernel,
        in_specs=[SMEM] + [VMEM] * (len(knowns) + len(extras) + 4),
        out_specs=(VMEM, VMEM),
        out_shape=(like, like),
        compiler_params=room(3),
    )(where, before, total, *knowns, *extras, high, low)


def assemble_kernel(pieces_ref, out_ref):
    for i in range(COLS):
        out_ref[pl.ds(i * 4, 4), :] = pieces_ref[i]


def assemble(pieces):
    return pl.pallas_call(
        assemble_kernel,
        in_specs=[VMEM],
        out_specs=VMEM,
        out_shape=jax.ShapeDtypeStruct((64, 1024), jnp.float32),
        compiler_params=room(2),
    )(pieces)


def finish_kernel(tiles_ref, near_ref, row_ref, pieces_ref, *refs):
    rhs_refs, (force_ref, solution_ref, residual_ref) = refs[:4], refs[4:]
    row = row_ref[0]
    for group in range(8):
        for half in range(2):
            solution_ref[pl.ds(group * 8, 8), pl.ds(half * 512, 512)] = pieces_ref[row * COLS + group * 2 + half]
    for t in range(2):
        own = tiles_ref[t]
        own_row = own // 8
        behind = (row // 2 - own_row // 2 + 4) % 4
        core = (row + own_row) % 2
        offset_own = pl.multiple_of((own % 8) * 128, 128)
        for distance in range(4):

            @pl.when(behind == distance)
            def _(distance=distance):
                residual_ref[t] = rhs_refs[distance][core, :, pl.ds(offset_own, 128)]

        total = residual_ref[t]
        for n in range(8):
            tile = near_ref[t, n]
            block = tile // 8
            half = (tile % 8) // 4
            offset = pl.multiple_of((tile % 4) * 128, 128)
            near = jnp.concatenate(
                [pieces_ref[block * COLS + group * 2 + half, :, pl.ds(offset, 128)] for group in range(8)], axis=0
            )
            total = total - three_pass(near, *split_bf16(force_ref[t, n]))
        residual_ref[t] = total


def finish(tile_list, neighbor_list, row, pieces, rhs, force):
    return pl.pallas_call(
        finish_kernel,
        out_shape=(
            jax.ShapeDtypeStruct((64, 1024), jnp.float32),
            jax.ShapeDtypeStruct((2, 64, 128), jnp.float32),
        ),
        in_specs=[SMEM, SMEM, SMEM] + [VMEM] * 6,
        out_specs=(VMEM, VMEM),
        compiler_params=room(8),
    )(tile_list, neighbor_list, row, pieces, *rhs, force)


def per_device(
    window_rhs,
    past_solution,
    past_panel,
    window_panel,
    diag_inverse,
    tile_list,
    neighbor_list,
    force_constants,
):
    row = lax.axis_index(PROW)
    col = lax.axis_index(PCOL)
    block = window_panel.reshape(-1, 128)
    where = jnp.stack([row, col]).astype(jnp.int32)
    inverse = diag_inverse[0]

    def onward(x):
        return lax.ppermute(x, "prow_0", [(i, (i + 1) % 4) for i in range(4)])

    other_rhs = lax.ppermute(window_rhs, "prow_1", [(0, 1), (1, 0)])
    pair = jnp.stack([window_rhs, other_rhs])
    next_rhs = onward(pair)
    past = product(past_solution, past_panel, 1, 1)
    past_rows = exchange(past.reshape(COLS, 4, 1024), PCOL)
    _, next_rhs = lax.optimization_barrier((past, next_rhs))
    far_rhs = onward(next_rhs)
    high, low = form(inverse, block)
    past_rows, high, far_rhs = lax.optimization_barrier((past_rows, high, far_rhs))
    last_rhs = onward(far_rhs)
    past_rows = past_rows.sum(axis=0)
    rhs_rows = lax.dynamic_slice_in_dim(window_rhs, col * 4, 4, 0)
    start_rows = start_product(rhs_rows, past_rows, inverse)
    start_rows = to_everyone(start_rows, PCOL, COLS)
    start_rows, last_rhs = lax.optimization_barrier((start_rows, last_rhs))
    full_rhs = [pair, next_rhs, far_rhs, last_rhs]
    start = assemble(start_rows)

    arrived = send(start, [(place(0, i), place(k, 0)) for i, k in ((0, 1), (1, 2), (3, 6), (4, 4))])
    relayed = send(arrived, [(place(k, 0), place(k + 1, 0)) for k in (2, 4, 6)])
    current, total = fire(0, where, start, start, [], [arrived, relayed], high, low)
    late = []
    for step in range(1, ROWS - 1):
        source = place(step, step - 1)
        beside = place(step ^ 1, step - 1)
        knowns = [send(current, [(source, place(step + 1, step))])]
        if step + 2 < ROWS:
            relayed = send(current, [(source, beside)])
            knowns += [send(relayed, [(beside, place(k, step))]) for k in range(step + 2, ROWS)]
        extras = late + [send(current, [(place(step + 1, step - 1), place(step + 1, step))])]
        late = []
        if step + 2 < ROWS:
            late = [send(current, [(place(k, step - 1), place(k, k - 1)) for k in range(step + 2, ROWS)])]
        current, total = fire(step, where, current, total, extras, knowns, high, low)

    pieces = current.reshape(8, 8, 2, 512).transpose(0, 2, 1, 3).reshape(COLS, 8, 512)
    spread = exchange(pieces, PCOL)
    own_piece = lax.dynamic_index_in_dim(spread, jnp.maximum(row - 1, 0), 0, keepdims=False)
    everything = to_everyone(own_piece, EVERY, ROWS * COLS)
    solution, residual = finish(
        tile_list[0], neighbor_list[0], where, everything, full_rhs, force_constants[0]
    )
    return (solution, residual[None])


def solution(mesh):
    torus = Mesh(mesh.devices.reshape(4, 2, 4, 4), EVERY)
    placed = (
        P(None, PROW),
        P(None, PCOL),
        P(PROW, PCOL),
        P(PROW, None, PCOL, None),
        P(PROW, None, None),
        P(EVERY, None),
        P(EVERY, None, None),
        P(EVERY, None, None, None, None),
    )
    return jax.shard_map(
        per_device,
        mesh=torus,
        in_specs=placed,
        out_specs=(P(None, PROW), P(EVERY, None, None, None)),
        check_vma=False,
    )
```

```python
import jax
import jax.numpy as jnp
from jax import lax
from jax.experimental import pallas as pl
from jax.experimental.pallas import tpu as pltpu
from jax.sharding import Mesh
from jax.sharding import PartitionSpec as P

PROW = ("prow_0", "prow_1")
PCOL = ("pcol_0", "pcol_1")
EVERY = ("prow_0", "prow_1", "pcol_0", "pcol_1")
ROWS = 8
COLS = 16
HIGH = lax.Precision.HIGH


def product(left, right, left_dim, right_dim):
    return lax.dot_general(
        left,
        right,
        (((left_dim,), (right_dim,)), ((), ())),
        precision=HIGH,
        preferred_element_type=jnp.float32,
    )


def exchange(pieces, axes):
    return lax.all_to_all(pieces, axes, 0, 0, tiled=True)


def to_everyone(x, axes, count):
    return exchange(jnp.broadcast_to(x[None], (count, *x.shape)), axes)


def place(row, col):
    return row * COLS + col


def send(x, pairs):
    return lax.ppermute(x, EVERY, pairs)


def split_bf16(x):
    high = x.astype(jnp.bfloat16)
    low = (x - high.astype(jnp.float32)).astype(jnp.bfloat16)
    return high, low


ACROSS = (((1,), (1,)), ((), ()))
ALONG = (((1,), (0,)), ((), ()))


def high_passes(left, right_high, dims):
    left_high, left_low = split_bf16(left)
    rows = left.shape[0]
    both = lax.dot_general(
        jnp.concatenate([left_high, left_low], axis=0), right_high, dims, preferred_element_type=jnp.float32
    )
    return both[:rows] + both[rows:]


def low_pass(left, right_low, dims):
    return lax.dot_general(left.astype(jnp.bfloat16), right_low, dims, preferred_element_type=jnp.float32)


def three_pass(left, right_high, right_low, dims=ACROSS):
    return high_passes(left, right_high, dims) + low_pass(left, right_low, dims)


VMEM = pl.BlockSpec(memory_space=pltpu.VMEM)
SMEM = pl.BlockSpec(memory_space=pltpu.SMEM)


def room(mib):
    return pltpu.CompilerParams(vmem_limit_bytes=mib * 1024 * 1024)


def in_hbm(x):
    return pltpu.with_memory_space_constraint(x, pltpu.HBM)


def in_vmem(x):
    return pltpu.with_memory_space_constraint(x, pltpu.VMEM)


PARTS = 4


def form_kernel(
    inverse_hbm,
    block_hbm,
    high_ref,
    low_ref,
    inverse_buffer,
    block_buffer,
    block_high_ref,
    block_low_ref,
    inverse_sems,
    block_sems,
):
    order = inverse_buffer.shape[0]
    part = order // PARTS
    lines = block_buffer.shape[0] // PARTS
    count = lines // part

    def block_copy(i):
        span = pl.ds(i * lines, lines)
        return pltpu.make_async_copy(block_hbm.at[span], block_buffer.at[span], block_sems.at[i])

    def inverse_copy(i):
        span = pl.ds(i * part, part)
        return pltpu.make_async_copy(inverse_hbm.at[span], inverse_buffer.at[span], inverse_sems.at[i])

    for i in range(PARTS):
        block_copy(i).start()
    for i in range(PARTS):
        inverse_copy(i).start()
    for i in range(PARTS):
        block_copy(i).wait()
        span = pl.ds(i * part, part)
        for j in range(count):
            lanes = pl.ds(j * 128, 128)
            strip = block_buffer[pl.ds(i * lines + j, part, stride=count), :]
            block_high_ref[span, lanes], block_low_ref[span, lanes] = split_bf16(strip)

    def one(a, b):
        return jnp.dot(a, b, preferred_element_type=jnp.float32)

    for i in range(PARTS):
        inverse_copy(i).wait()
        span = pl.ds(i * part, part)
        inverse_high, inverse_low = split_bf16(inverse_buffer[span, :])
        total = one(inverse_high, block_high_ref[...])
        total = total + one(inverse_high, block_low_ref[...])
        total = total + one(inverse_low, block_high_ref[...])
        high_ref[:, span], low_ref[:, span] = split_bf16(total.T)


def form(inverse, block):
    order = inverse.shape[0]
    half = jax.ShapeDtypeStruct((order, order), jnp.bfloat16)
    hbm = pl.BlockSpec(memory_space=pltpu.HBM)
    return pl.pallas_call(
        form_kernel,
        in_specs=[hbm, hbm],
        out_specs=(VMEM,) * 2,
        out_shape=(half,) * 2,
        scratch_shapes=[
            pltpu.VMEM(inverse.shape, jnp.float32),
            pltpu.VMEM(block.shape, jnp.float32),
            pltpu.VMEM((order, order), jnp.bfloat16),
            pltpu.VMEM((order, order), jnp.bfloat16),
            pltpu.SemaphoreType.DMA((PARTS,)),
            pltpu.SemaphoreType.DMA((PARTS,)),
        ],
        compiler_params=room(24),
    )(in_hbm(inverse), in_hbm(block))


def start_kernel(rhs_ref, past_ref, inverse_hbm, out_ref, buffer, sems):
    part = buffer.shape[0] // PARTS

    def copy(i):
        span = pl.ds(i * part, part)
        return pltpu.make_async_copy(inverse_hbm.at[span], buffer.at[span], sems.at[i])

    for i in range(PARTS):
        copy(i).start()
    diff = rhs_ref[...] - past_ref[...]
    for i in range(PARTS):
        copy(i).wait()
        span = pl.ds(i * part, part)
        out_ref[:, span] = three_pass(diff, *split_bf16(buffer[span, :]))


def start_product(rhs, past, inverse):
    return pl.pallas_call(
        start_kernel,
        in_specs=[VMEM, VMEM, pl.BlockSpec(memory_space=pltpu.HBM)],
        out_specs=VMEM,
        out_shape=jax.ShapeDtypeStruct(rhs.shape, jnp.float32),
        scratch_shapes=[pltpu.VMEM(inverse.shape, jnp.float32), pltpu.SemaphoreType.DMA((PARTS,))],
        compiler_params=room(12),
    )(rhs, past, in_hbm(inverse))


def fire(step, where, before, total, extra, knowns, high, low):
    def kernel(where_ref, before_ref, total_ref, *refs):
        row, col = where_ref[0], where_ref[1]
        turn = jnp.logical_and(col == step, row > step)
        known_refs = refs[: len(knowns)]
        extra_refs = refs[len(knowns) : -4]
        high_ref, low_ref, out_ref, sum_ref = refs[-4:]
        if extra_refs:
            sum_ref[...] = total_ref[...] + extra_refs[0][...]
        else:
            sum_ref[...] = jnp.where(row == col + 1, total_ref[...], 0.0)

        @pl.when(jnp.logical_not(turn))
        def _():
            out_ref[...] = before_ref[...]

        @pl.when(jnp.logical_and(turn, row == step + 1))
        def _():
            out_ref[...] = known_refs[0][...]

        @pl.when(jnp.logical_and(turn, row > step + 1))
        def _():
            known = known_refs[0][...]
            for ref in known_refs[1:]:
                known = known + ref[...]
            out_ref[...] = known

        @pl.when(turn)
        def _():
            out_ref[...] = sum_ref[...] - three_pass(out_ref[...], high_ref[...], low_ref[...], ALONG)

    extras = [] if extra is None else [extra]
    like = jax.ShapeDtypeStruct(before.shape, jnp.float32)
    return pl.pallas_call(
        kernel,
        in_specs=[SMEM] + [VMEM] * (len(knowns) + len(extras) + 4),
        out_specs=(VMEM, VMEM),
        out_shape=(like, like),
        compiler_params=room(3),
    )(where, before, total, *knowns, *extras, high, low)


def assemble_kernel(pieces_ref, out_ref):
    for i in range(COLS):
        out_ref[pl.ds(i * 4, 4), :] = pieces_ref[i]


def assemble(pieces):
    return pl.pallas_call(
        assemble_kernel,
        in_specs=[VMEM],
        out_specs=VMEM,
        out_shape=jax.ShapeDtypeStruct((64, 1024), jnp.float32),
        compiler_params=room(2),
    )(pieces)


def finish_kernel(tiles_ref, near_ref, row_ref, pieces_ref, rhs_ref, force_ref, solution_ref, residual_ref):
    row = row_ref[0]
    for group in range(8):
        for half in range(2):
            solution_ref[pl.ds(group * 8, 8), pl.ds(half * 512, 512)] = pieces_ref[row * COLS + group * 2 + half]
    for t in range(2):
        own = tiles_ref[t]
        total = rhs_ref[own // 8, :, pl.ds(pl.multiple_of((own % 8) * 128, 128), 128)]
        for n in range(8):
            tile = near_ref[t, n]
            block = tile // 8
            half = (tile % 8) // 4
            offset = pl.multiple_of((tile % 4) * 128, 128)
            near = jnp.concatenate(
                [pieces_ref[block * COLS + group * 2 + half, :, pl.ds(offset, 128)] for group in range(8)], axis=0
            )
            total = total - three_pass(near, *split_bf16(force_ref[t, n]))
        residual_ref[t] = total


def finish(tile_list, neighbor_list, row, pieces, rhs, force):
    return pl.pallas_call(
        finish_kernel,
        out_shape=(
            jax.ShapeDtypeStruct((64, 1024), jnp.float32),
            jax.ShapeDtypeStruct((2, 64, 128), jnp.float32),
        ),
        in_specs=[SMEM, SMEM, SMEM] + [VMEM] * 3,
        out_specs=(VMEM, VMEM),
        compiler_params=room(8),
    )(tile_list, neighbor_list, row, pieces, rhs, force)


def per_device(
    window_rhs,
    past_solution,
    past_panel,
    window_panel,
    diag_inverse,
    tile_list,
    neighbor_list,
    force_constants,
):
    row = lax.axis_index(PROW)
    col = lax.axis_index(PCOL)
    block = window_panel.reshape(-1, 128)
    where = jnp.stack([row, col]).astype(jnp.int32)
    inverse = diag_inverse[0]

    full_rhs = lax.all_gather(window_rhs, PROW, axis=0, tiled=False)
    past = product(past_solution, past_panel, 1, 1)
    past_rows = exchange(past.reshape(COLS, 4, 1024), PCOL).sum(axis=0)
    high, low = (in_vmem(x) for x in form(inverse, block))
    past_rows, high = lax.optimization_barrier((past_rows, high))
    rhs_rows = lax.dynamic_slice_in_dim(window_rhs, col * 4, 4, 0)
    start_rows = start_product(rhs_rows, past_rows, inverse)
    start = assemble(to_everyone(start_rows, PCOL, COLS))

    arrived = send(start, [(place(0, k - 1), place(k, 0)) for k in range(1, ROWS)])
    current, total = fire(0, where, start, start, None, [arrived], high, low)
    for step in range(1, ROWS - 1):
        source = place(step, step - 1)
        beside = place(step ^ 1, step - 1)
        knowns = [send(current, [(source, place(step + 1, step))])]
        if step + 2 < ROWS:
            relayed = send(current, [(source, beside)])
            knowns += [send(relayed, [(beside, place(k, step))]) for k in range(step + 2, ROWS)]
        extra = send(current, [(place(k, step - 1), place(k, k - 1)) for k in range(step + 1, ROWS)])
        current, total = fire(step, where, current, total, extra, knowns, high, low)

    pieces = current.reshape(8, 8, 2, 512).transpose(0, 2, 1, 3).reshape(COLS, 8, 512)
    spread = exchange(pieces, PCOL)
    own_piece = lax.dynamic_index_in_dim(spread, jnp.maximum(row - 1, 0), 0, keepdims=False)
    everything = to_everyone(own_piece, EVERY, ROWS * COLS)
    solution, residual = finish(
        tile_list[0], neighbor_list[0], where, everything, full_rhs, force_constants[0]
    )
    return (solution, residual[None])


def solution(mesh):
    torus = Mesh(mesh.devices.reshape(4, 2, 4, 4), EVERY)
    placed = (
        P(None, PROW),
        P(None, PCOL),
        P(PROW, PCOL),
        P(PROW, None, PCOL, None),
        P(PROW, None, None),
        P(EVERY, None),
        P(EVERY, None, None),
        P(EVERY, None, None, None, None),
    )
    return jax.shard_map(
        per_device,
        mesh=torus,
        in_specs=placed,
        out_specs=(P(None, PROW), P(EVERY, None, None, None)),
        check_vma=False,
    )
```

```python
import jax
import jax.numpy as jnp
from jax import lax
from jax.experimental import pallas as pl
from jax.experimental.pallas import tpu as pltpu
from jax.sharding import Mesh
from jax.sharding import PartitionSpec as P

PROW = ("prow_0", "prow_1")
PCOL = ("pcol_0", "pcol_1")
EVERY = ("prow_0", "prow_1", "pcol_0", "pcol_1")
ROWS = 8
COLS = 16
HIGH = lax.Precision.HIGH


def product(left, right, left_dim, right_dim):
    return lax.dot_general(
        left,
        right,
        (((left_dim,), (right_dim,)), ((), ())),
        precision=HIGH,
        preferred_element_type=jnp.float32,
    )


def exchange(pieces, axes):
    return lax.all_to_all(pieces, axes, 0, 0, tiled=True)


def to_everyone(x, axes, count):
    return exchange(jnp.broadcast_to(x[None], (count, *x.shape)), axes)


def place(row, col):
    return row * COLS + col


def send(x, pairs):
    return lax.ppermute(x, EVERY, pairs)


def split_bf16(x):
    high = x.astype(jnp.bfloat16)
    low = (x - high.astype(jnp.float32)).astype(jnp.bfloat16)
    return high, low


ACROSS = (((1,), (1,)), ((), ()))
ALONG = (((1,), (0,)), ((), ()))


def high_passes(left, right_high, dims):
    left_high, left_low = split_bf16(left)
    rows = left.shape[0]
    both = lax.dot_general(
        jnp.concatenate([left_high, left_low], axis=0), right_high, dims, preferred_element_type=jnp.float32
    )
    return both[:rows] + both[rows:]


def low_pass(left, right_low, dims):
    return lax.dot_general(left.astype(jnp.bfloat16), right_low, dims, preferred_element_type=jnp.float32)


def three_pass(left, right_high, right_low, dims=ACROSS):
    return high_passes(left, right_high, dims) + low_pass(left, right_low, dims)


VMEM = pl.BlockSpec(memory_space=pltpu.VMEM)
SMEM = pl.BlockSpec(memory_space=pltpu.SMEM)


def room(mib):
    return pltpu.CompilerParams(vmem_limit_bytes=mib * 1024 * 1024)


def in_hbm(x):
    return pltpu.with_memory_space_constraint(x, pltpu.HBM)


def in_vmem(x):
    return pltpu.with_memory_space_constraint(x, pltpu.VMEM)


PARTS = 4


def form_kernel(
    inverse_hbm,
    block_hbm,
    high_ref,
    low_ref,
    inverse_buffer,
    block_buffer,
    block_high_ref,
    block_low_ref,
    inverse_sems,
    block_sems,
):
    order = inverse_buffer.shape[0]
    part = order // PARTS
    lines = block_buffer.shape[0] // PARTS
    count = lines // part

    def block_copy(i):
        span = pl.ds(i * lines, lines)
        return pltpu.make_async_copy(block_hbm.at[span], block_buffer.at[span], block_sems.at[i])

    def inverse_copy(i):
        span = pl.ds(i * part, part)
        return pltpu.make_async_copy(inverse_hbm.at[span], inverse_buffer.at[span], inverse_sems.at[i])

    for i in range(PARTS):
        block_copy(i).start()
    for i in range(PARTS):
        inverse_copy(i).start()
    for i in range(PARTS):
        block_copy(i).wait()
        span = pl.ds(i * part, part)
        for j in range(count):
            lanes = pl.ds(j * 128, 128)
            strip = block_buffer[pl.ds(i * lines + j, part, stride=count), :]
            block_high_ref[span, lanes], block_low_ref[span, lanes] = split_bf16(strip)

    def one(a, b):
        return jnp.dot(a, b, preferred_element_type=jnp.float32)

    for i in range(PARTS):
        inverse_copy(i).wait()
        span = pl.ds(i * part, part)
        inverse_high, inverse_low = split_bf16(inverse_buffer[span, :])
        total = one(inverse_high, block_high_ref[...])
        total = total + one(inverse_high, block_low_ref[...])
        total = total + one(inverse_low, block_high_ref[...])
        high_ref[:, span], low_ref[:, span] = split_bf16(total.T)


def form(inverse, block):
    order = inverse.shape[0]
    half = jax.ShapeDtypeStruct((order, order), jnp.bfloat16)
    hbm = pl.BlockSpec(memory_space=pltpu.HBM)
    return pl.pallas_call(
        form_kernel,
        in_specs=[hbm, hbm],
        out_specs=(VMEM,) * 2,
        out_shape=(half,) * 2,
        scratch_shapes=[
            pltpu.VMEM(inverse.shape, jnp.float32),
            pltpu.VMEM(block.shape, jnp.float32),
            pltpu.VMEM((order, order), jnp.bfloat16),
            pltpu.VMEM((order, order), jnp.bfloat16),
            pltpu.SemaphoreType.DMA((PARTS,)),
            pltpu.SemaphoreType.DMA((PARTS,)),
        ],
        compiler_params=room(24),
    )(in_hbm(inverse), in_hbm(block))


def start_kernel(rhs_ref, past_ref, inverse_hbm, out_ref, buffer, sems):
    part = buffer.shape[0] // PARTS

    def copy(i):
        span = pl.ds(i * part, part)
        return pltpu.make_async_copy(inverse_hbm.at[span], buffer.at[span], sems.at[i])

    for i in range(PARTS):
        copy(i).start()
    diff = rhs_ref[...] - past_ref[...]
    for i in range(PARTS):
        copy(i).wait()
        span = pl.ds(i * part, part)
        out_ref[:, span] = three_pass(diff, *split_bf16(buffer[span, :]))


def start_product(rhs, past, inverse):
    return pl.pallas_call(
        start_kernel,
        in_specs=[VMEM, VMEM, pl.BlockSpec(memory_space=pltpu.HBM)],
        out_specs=VMEM,
        out_shape=jax.ShapeDtypeStruct(rhs.shape, jnp.float32),
        scratch_shapes=[pltpu.VMEM(inverse.shape, jnp.float32), pltpu.SemaphoreType.DMA((PARTS,))],
        compiler_params=room(12),
    )(rhs, past, in_hbm(inverse))


def fire(step, where, before, base, knowns, high, low):
    def kernel(where_ref, before_ref, base_ref, *refs):
        known_refs = refs[:-3]
        high_ref, low_ref, out_ref = refs[-3:]
        row, col = where_ref[0], where_ref[1]
        turn = jnp.logical_and(col == step, row > step)

        @pl.when(jnp.logical_not(turn))
        def _():
            out_ref[...] = before_ref[...]

        @pl.when(jnp.logical_and(turn, row == step + 1))
        def _():
            out_ref[...] = known_refs[0][...]

        @pl.when(jnp.logical_and(turn, row > step + 1))
        def _():
            known = known_refs[0][...]
            for ref in known_refs[1:]:
                known = known + ref[...]
            out_ref[...] = known

        @pl.when(turn)
        def _():
            out_ref[...] = base_ref[...] - three_pass(out_ref[...], high_ref[...], low_ref[...], ALONG)

    return pl.pallas_call(
        kernel,
        in_specs=[SMEM] + [VMEM] * (len(knowns) + 4),
        out_specs=VMEM,
        out_shape=jax.ShapeDtypeStruct(before.shape, jnp.float32),
        compiler_params=room(3),
    )(where, before, base, *knowns, high, low)


def assemble_kernel(pieces_ref, out_ref):
    for i in range(COLS):
        out_ref[pl.ds(i * 4, 4), :] = pieces_ref[i]


def assemble(pieces):
    return pl.pallas_call(
        assemble_kernel,
        in_specs=[VMEM],
        out_specs=VMEM,
        out_shape=jax.ShapeDtypeStruct((64, 1024), jnp.float32),
        compiler_params=room(2),
    )(pieces)


def finish_kernel(tiles_ref, near_ref, row_ref, pieces_ref, rhs_ref, force_ref, solution_ref, residual_ref):
    row = row_ref[0]
    for group in range(8):
        for half in range(2):
            solution_ref[pl.ds(group * 8, 8), pl.ds(half * 512, 512)] = pieces_ref[row * COLS + group * 2 + half]
    for t in range(2):
        own = tiles_ref[t]
        total = rhs_ref[own // 8, :, pl.ds(pl.multiple_of((own % 8) * 128, 128), 128)]
        for n in range(8):
            tile = near_ref[t, n]
            block = tile // 8
            half = (tile % 8) // 4
            offset = pl.multiple_of((tile % 4) * 128, 128)
            near = jnp.concatenate(
                [pieces_ref[block * COLS + group * 2 + half, :, pl.ds(offset, 128)] for group in range(8)], axis=0
            )
            total = total - three_pass(near, *split_bf16(force_ref[t, n]))
        residual_ref[t] = total


def finish(tile_list, neighbor_list, row, pieces, rhs, force):
    return pl.pallas_call(
        finish_kernel,
        out_shape=(
            jax.ShapeDtypeStruct((64, 1024), jnp.float32),
            jax.ShapeDtypeStruct((2, 64, 128), jnp.float32),
        ),
        in_specs=[SMEM, SMEM, SMEM] + [VMEM] * 3,
        out_specs=(VMEM, VMEM),
        compiler_params=room(8),
    )(tile_list, neighbor_list, row, pieces, rhs, force)


def per_device(
    window_rhs,
    past_solution,
    past_panel,
    window_panel,
    diag_inverse,
    tile_list,
    neighbor_list,
    force_constants,
):
    row = lax.axis_index(PROW)
    col = lax.axis_index(PCOL)
    block = window_panel.reshape(-1, 128)
    where = jnp.stack([row, col]).astype(jnp.int32)
    inverse = diag_inverse[0]

    full_rhs = lax.all_gather(window_rhs, PROW, axis=0, tiled=False)
    past = product(past_solution, past_panel, 1, 1)
    past_rows = exchange(past.reshape(COLS, 4, 1024), PCOL).sum(axis=0)
    high, low = (in_vmem(x) for x in form(inverse, block))
    past_rows, high = lax.optimization_barrier((past_rows, high))
    rhs_rows = lax.dynamic_slice_in_dim(window_rhs, col * 4, 4, 0)
    start_rows = start_product(rhs_rows, past_rows, inverse)
    start = assemble(to_everyone(start_rows, PCOL, COLS))

    arrived = send(start, [(place(0, k - 1), place(k, 0)) for k in range(1, ROWS)])
    current = fire(0, where, start, start, [arrived], high, low)
    for step in range(1, ROWS - 1):
        source = place(step, step - 1)
        knowns = [send(current, [(source, place(k, step))]) for k in range(step + 1, ROWS)]
        partial = send(current, [(place(k, step - 1), place(k, step)) for k in range(step + 1, ROWS)])
        current = fire(step, where, current, partial, knowns, high, low)

    pieces = current.reshape(8, 8, 2, 512).transpose(0, 2, 1, 3).reshape(COLS, 8, 512)
    spread = exchange(pieces, PCOL)
    own_piece = lax.dynamic_index_in_dim(spread, jnp.maximum(row - 1, 0), 0, keepdims=False)
    everything = to_everyone(own_piece, EVERY, ROWS * COLS)
    solution, residual = finish(
        tile_list[0], neighbor_list[0], where, everything, full_rhs, force_constants[0]
    )
    return (solution, residual[None])


def solution(mesh):
    torus = Mesh(mesh.devices.reshape(4, 2, 4, 4), EVERY)
    placed = (
        P(None, PROW),
        P(None, PCOL),
        P(PROW, PCOL),
        P(PROW, None, PCOL, None),
        P(PROW, None, None),
        P(EVERY, None),
        P(EVERY, None, None),
        P(EVERY, None, None, None, None),
    )
    return jax.shard_map(
        per_device,
        mesh=torus,
        in_specs=placed,
        out_specs=(P(None, PROW), P(EVERY, None, None, None)),
        check_vma=False,
    )
```

```python
import jax
import jax.numpy as jnp
from jax import lax
from jax.experimental import pallas as pl
from jax.experimental.pallas import tpu as pltpu
from jax.sharding import Mesh
from jax.sharding import PartitionSpec as P

PROW = ("prow_0", "prow_1")
PCOL = ("pcol_0", "pcol_1")
EVERY = ("prow_0", "prow_1", "pcol_0", "pcol_1")
ROWS = 8
COLS = 16
HIGH = lax.Precision.HIGH


def product(left, right, left_dim, right_dim):
    return lax.dot_general(
        left,
        right,
        (((left_dim,), (right_dim,)), ((), ())),
        precision=HIGH,
        preferred_element_type=jnp.float32,
    )


def exchange(pieces, axes):
    return lax.all_to_all(pieces, axes, 0, 0, tiled=True)


def to_everyone(x, axes, count):
    return exchange(jnp.broadcast_to(x[None], (count, *x.shape)), axes)


def place(row, col):
    return row * COLS + col


def send(x, pairs):
    return lax.ppermute(x, EVERY, pairs)


def split_bf16(x):
    high = x.astype(jnp.bfloat16)
    low = (x - high.astype(jnp.float32)).astype(jnp.bfloat16)
    return high, low


ACROSS = (((1,), (1,)), ((), ()))
ALONG = (((1,), (0,)), ((), ()))


def high_passes(left, right_high, dims):
    left_high, left_low = split_bf16(left)
    rows = left.shape[0]
    both = lax.dot_general(
        jnp.concatenate([left_high, left_low], axis=0), right_high, dims, preferred_element_type=jnp.float32
    )
    return both[:rows] + both[rows:]


def low_pass(left, right_low, dims):
    return lax.dot_general(left.astype(jnp.bfloat16), right_low, dims, preferred_element_type=jnp.float32)


def three_pass(left, right_high, right_low, dims=ACROSS):
    return high_passes(left, right_high, dims) + low_pass(left, right_low, dims)


VMEM = pl.BlockSpec(memory_space=pltpu.VMEM)
SMEM = pl.BlockSpec(memory_space=pltpu.SMEM)


def room(mib):
    return pltpu.CompilerParams(vmem_limit_bytes=mib * 1024 * 1024)


def in_hbm(x):
    return pltpu.with_memory_space_constraint(x, pltpu.HBM)


def in_vmem(x):
    return pltpu.with_memory_space_constraint(x, pltpu.VMEM)


PARTS = 4


def form_kernel(
    inverse_hbm,
    block_hbm,
    high_ref,
    low_ref,
    inverse_buffer,
    block_buffer,
    block_high_ref,
    block_low_ref,
    inverse_sems,
    block_sems,
):
    order = inverse_buffer.shape[0]
    part = order // PARTS
    lines = block_buffer.shape[0] // PARTS
    count = lines // part

    def block_copy(i):
        span = pl.ds(i * lines, lines)
        return pltpu.make_async_copy(block_hbm.at[span], block_buffer.at[span], block_sems.at[i])

    def inverse_copy(i):
        span = pl.ds(i * part, part)
        return pltpu.make_async_copy(inverse_hbm.at[span], inverse_buffer.at[span], inverse_sems.at[i])

    for i in range(PARTS):
        block_copy(i).start()
    for i in range(PARTS):
        inverse_copy(i).start()
    for i in range(PARTS):
        block_copy(i).wait()
        span = pl.ds(i * part, part)
        for j in range(count):
            lanes = pl.ds(j * 128, 128)
            strip = block_buffer[pl.ds(i * lines + j, part, stride=count), :]
            block_high_ref[span, lanes], block_low_ref[span, lanes] = split_bf16(strip)

    def one(a, b):
        return jnp.dot(a, b, preferred_element_type=jnp.float32)

    for i in range(PARTS):
        inverse_copy(i).wait()
        span = pl.ds(i * part, part)
        inverse_high, inverse_low = split_bf16(inverse_buffer[span, :])
        total = one(inverse_high, block_high_ref[...])
        total = total + one(inverse_high, block_low_ref[...])
        total = total + one(inverse_low, block_high_ref[...])
        high_ref[:, span], low_ref[:, span] = split_bf16(total.T)


def form(inverse, block):
    order = inverse.shape[0]
    half = jax.ShapeDtypeStruct((order, order), jnp.bfloat16)
    hbm = pl.BlockSpec(memory_space=pltpu.HBM)
    return pl.pallas_call(
        form_kernel,
        in_specs=[hbm, hbm],
        out_specs=(VMEM,) * 2,
        out_shape=(half,) * 2,
        scratch_shapes=[
            pltpu.VMEM(inverse.shape, jnp.float32),
            pltpu.VMEM(block.shape, jnp.float32),
            pltpu.VMEM((order, order), jnp.bfloat16),
            pltpu.VMEM((order, order), jnp.bfloat16),
            pltpu.SemaphoreType.DMA((PARTS,)),
            pltpu.SemaphoreType.DMA((PARTS,)),
        ],
        compiler_params=room(24),
    )(in_hbm(inverse), in_hbm(block))


def start_kernel(rhs_ref, past_ref, inverse_hbm, out_ref, buffer, sems):
    part = buffer.shape[0] // PARTS

    def copy(i):
        span = pl.ds(i * part, part)
        return pltpu.make_async_copy(inverse_hbm.at[span], buffer.at[span], sems.at[i])

    for i in range(PARTS):
        copy(i).start()
    diff = rhs_ref[...] - past_ref[...]
    for i in range(PARTS):
        copy(i).wait()
        span = pl.ds(i * part, part)
        out_ref[:, span] = three_pass(diff, *split_bf16(buffer[span, :]))


def start_product(rhs, past, inverse):
    return pl.pallas_call(
        start_kernel,
        in_specs=[VMEM, VMEM, pl.BlockSpec(memory_space=pltpu.HBM)],
        out_specs=VMEM,
        out_shape=jax.ShapeDtypeStruct(rhs.shape, jnp.float32),
        scratch_shapes=[pltpu.VMEM(inverse.shape, jnp.float32), pltpu.SemaphoreType.DMA((PARTS,))],
        compiler_params=room(12),
    )(rhs, past, in_hbm(inverse))


def fire(step, where, before, base, knowns, high, low):
    def kernel(where_ref, before_ref, base_ref, *refs):
        known_refs = refs[:-3]
        high_ref, low_ref, out_ref = refs[-3:]
        row, col = where_ref[0], where_ref[1]
        turn = jnp.logical_and(col == step, row > step)

        @pl.when(jnp.logical_not(turn))
        def _():
            out_ref[...] = before_ref[...]

        @pl.when(jnp.logical_and(turn, row == step + 1))
        def _():
            out_ref[...] = known_refs[0][...]

        @pl.when(jnp.logical_and(turn, row > step + 1))
        def _():
            known = known_refs[0][...]
            for ref in known_refs[1:]:
                known = known + ref[...]
            out_ref[...] = known

        @pl.when(turn)
        def _():
            out_ref[...] = base_ref[...] - three_pass(out_ref[...], high_ref[...], low_ref[...], ALONG)

    return pl.pallas_call(
        kernel,
        in_specs=[SMEM] + [VMEM] * (len(knowns) + 4),
        out_specs=VMEM,
        out_shape=jax.ShapeDtypeStruct(before.shape, jnp.float32),
        compiler_params=room(3),
    )(where, before, base, *knowns, high, low)


def assemble_kernel(pieces_ref, out_ref):
    for i in range(COLS):
        out_ref[pl.ds(i * 4, 4), :] = pieces_ref[i]


def assemble(pieces):
    return pl.pallas_call(
        assemble_kernel,
        in_specs=[VMEM],
        out_specs=VMEM,
        out_shape=jax.ShapeDtypeStruct((64, 1024), jnp.float32),
        compiler_params=room(2),
    )(pieces)


def finish_kernel(tiles_ref, near_ref, row_ref, pieces_ref, rhs_ref, force_ref, solution_ref, residual_ref):
    row = row_ref[0]
    for group in range(8):
        for half in range(2):
            solution_ref[pl.ds(group * 8, 8), pl.ds(half * 512, 512)] = pieces_ref[row * COLS + group * 2 + half]
    for t in range(2):
        own = tiles_ref[t]
        total = rhs_ref[own // 8, :, pl.ds(pl.multiple_of((own % 8) * 128, 128), 128)]
        for n in range(8):
            tile = near_ref[t, n]
            block = tile // 8
            half = (tile % 8) // 4
            offset = pl.multiple_of((tile % 4) * 128, 128)
            near = jnp.concatenate(
                [pieces_ref[block * COLS + group * 2 + half, :, pl.ds(offset, 128)] for group in range(8)], axis=0
            )
            total = total - three_pass(near, *split_bf16(force_ref[t, n]))
        residual_ref[t] = total


def finish(tile_list, neighbor_list, row, pieces, rhs, force):
    return pl.pallas_call(
        finish_kernel,
        out_shape=(
            jax.ShapeDtypeStruct((64, 1024), jnp.float32),
            jax.ShapeDtypeStruct((2, 64, 128), jnp.float32),
        ),
        in_specs=[SMEM, SMEM, SMEM] + [VMEM] * 3,
        out_specs=(VMEM, VMEM),
        compiler_params=room(8),
    )(tile_list, neighbor_list, row, pieces, rhs, force)


def per_device(
    window_rhs,
    past_solution,
    past_panel,
    window_panel,
    diag_inverse,
    tile_list,
    neighbor_list,
    force_constants,
):
    row = lax.axis_index(PROW)
    col = lax.axis_index(PCOL)
    block = window_panel.reshape(-1, 128)
    where = jnp.stack([row, col]).astype(jnp.int32)
    inverse = diag_inverse[0]

    full_rhs = lax.all_gather(window_rhs, PROW, axis=0, tiled=False)
    past = product(past_solution, past_panel, 1, 1)
    past_rows = exchange(past.reshape(COLS, 4, 1024), PCOL).sum(axis=0)
    high, low = (in_vmem(x) for x in form(inverse, block))
    past_rows, high = lax.optimization_barrier((past_rows, high))
    rhs_rows = lax.dynamic_slice_in_dim(window_rhs, col * 4, 4, 0)
    start_rows = start_product(rhs_rows, past_rows, inverse)
    start = assemble(to_everyone(start_rows, PCOL, COLS))

    arrived = send(start, [(place(0, k - 1), place(k, 0)) for k in range(1, ROWS)])
    current = fire(0, where, start, start, [arrived], high, low)
    for step in range(1, ROWS - 1):
        source = place(step, step - 1)
        knowns = [send(current, [(source, place(k, step))]) for k in range(step + 1, ROWS)]
        partial = send(current, [(place(k, step - 1), place(k, step)) for k in range(step + 1, ROWS)])
        current = fire(step, where, current, partial, knowns, high, low)
        if step == 3:
            current, full_rhs = lax.optimization_barrier((current, full_rhs))

    pieces = current.reshape(8, 8, 2, 512).transpose(0, 2, 1, 3).reshape(COLS, 8, 512)
    spread = exchange(pieces, PCOL)
    own_piece = lax.dynamic_index_in_dim(spread, jnp.maximum(row - 1, 0), 0, keepdims=False)
    everything = to_everyone(own_piece, EVERY, ROWS * COLS)
    solution, residual = finish(
        tile_list[0], neighbor_list[0], where, everything, full_rhs, force_constants[0]
    )
    return (solution, residual[None])


def solution(mesh):
    torus = Mesh(mesh.devices.reshape(4, 2, 4, 4), EVERY)
    placed = (
        P(None, PROW),
        P(None, PCOL),
        P(PROW, PCOL),
        P(PROW, None, PCOL, None),
        P(PROW, None, None),
        P(EVERY, None),
        P(EVERY, None, None),
        P(EVERY, None, None, None, None),
    )
    return jax.shard_map(
        per_device,
        mesh=torus,
        in_specs=placed,
        out_specs=(P(None, PROW), P(EVERY, None, None, None)),
        check_vma=False,
    )
```
